256 devices in a mesh: traj: 32 (over z, y), seg: 8 (over x, core).
Axes of the slice: x: 4, y: 4, z: 8, core: 2. Of those that a mesh axis runs over, the one named last changes fastest.
Arguments:
- coords: float32 [32, 1024, 3, 512], P('traj', 'seg')
- pairs: int32 [2, 1024], replicated, may hold values from 0 to 511, as said below
- lengths: int32 [32], P('traj'), may hold values from 1 to 1024, 24576 in all
Outputs:
- projected: float32 [32, 1024, 128], P('traj', 'seg')
The draws below stay inside these ranges and needn't reach their ends.
Inputs may be any that keep to these rules, and one draw needn't show every extreme that they name: `pairs`: atom indices; the two atoms of a contact differ. `lengths`: each trajectory's recorded frames fill its first slots.
All inputs are finite; a program needn't handle non-finite values. No bound on the sum of `lengths` on one device may be relied on, other than what follows from the above.
Results may differ from the reference program's by a relative error of at most 0.0003.
Values sent between devices are 32-bit elements; how exact they have to be, the bound alone decides.
No kernel may reach another device: no remote copies, remote signals or barrier semaphores. Data moves between devices by JAX's collectives and lax.ppermute only.
A program may use at most 128 MiB of HBM per device.

```python
import math
import jax
import jax.numpy as jnp
import numpy as np
from jax import lax

FEAT = 1024
K = 128
ATOMS = 512
LAG = 10
ITERS = 3
TRAJS = 32
SEG_LEN = 1024


def draw_coords(key, part):
    keys = jax.random.split(jax.random.fold_in(key, 7), 6)
    shared_base = jax.random.normal(keys[0], (1, 1, 3, ATOMS), jnp.float32) * 1.5
    own_base = jax.random.normal(keys[1], (TRAJS, 1, 3, ATOMS), jnp.float32) * 0.3
    amplitude = jax.random.uniform(keys[2], (TRAJS, 1, 3, ATOMS), jnp.float32, 0.2, 0.8)
    log_freq = jax.random.uniform(keys[3], (1, 1, 1, ATOMS), jnp.float32, math.log(0.005), math.log(0.1))
    phase = jax.random.uniform(keys[4], (TRAJS, 1, 3, ATOMS), jnp.float32, -math.pi, math.pi)
    times = jnp.arange(SEG_LEN, dtype=jnp.float32).reshape(1, SEG_LEN, 1, 1)
    shape = (TRAJS, SEG_LEN, 3, ATOMS)
    noise = jax.random.normal(keys[5], shape, jnp.float32) * 0.3
    motion = amplitude * jnp.sin(jnp.exp(log_freq) * times + phase)
    return shared_base + own_base + motion + noise


def draw_pairs(key, part):
    keys = jax.random.split(jax.random.fold_in(key, 11), 2)
    first_atom = jax.random.randint(keys[0], (FEAT,), 0, ATOMS, jnp.int32)
    offset = jax.random.randint(keys[1], (FEAT,), 1, ATOMS, jnp.int32)
    second_atom = (first_atom + offset) % ATOMS
    first_atom = first_atom.at[0].set(0)
    second_atom = second_atom.at[0].set(ATOMS - 1)
    return jnp.stack([first_atom, second_atom]).astype(jnp.int32)


def profile(number_of, total, reach, slope):
    loads = [(1 << 20) // math.isqrt(standing ** slope) + 1 for standing in range(2, number_of + 1)]
    spare, given = total - reach - (number_of - 1), [1] * (number_of - 1)
    while spare > 0:
        movable = [i for i in range(number_of - 1) if given[i] < reach]
        whole, left = sum([loads[i] for i in movable]), spare
        for i in movable:
            more = min(reach - given[i], max(1, left * loads[i] // whole), spare)
            given[i] = given[i] + more
            spare = spare - more
    return np.array([reach] + given)


def uneven(key, amount, total, limit, skew):
    if amount == 2:
        one = jax.random.randint(key, (), max(1, total - limit), min(limit, total - 1) + 1)
        return jnp.stack([one, total - one])
    tallies = jnp.asarray(profile(amount, total, limit, skew), jnp.int32)
    couples = (amount - 1) // 2
    source_of, sink = tallies[1:1 + 2 * couples:2], tallies[2:2 + 2 * couples:2]
    slack = jnp.minimum(source_of - 1, limit - sink)
    passed = jax.random.randint(jax.random.fold_in(key, 1), (couples,), 0, 1 << 20) % (slack + 1)
    tallies = tallies.at[1:1 + 2 * couples:2].set(source_of - passed).at[2:2 + 2 * couples:2].set(sink + passed)
    return tallies[jax.random.permutation(jax.random.fold_in(key, 2), amount)]


def setup_inputs(seed: int = 0) -> dict:
    splits = jax.random.split(jax.random.key(seed), 4)
    return {
        "coords": draw_coords(jax.random.fold_in(splits[3], 71), 0),
        "pairs": draw_pairs(jax.random.fold_in(splits[3], 71), 0),
        "lengths": uneven(splits[2], TRAJS, TRAJS * SEG_LEN * 3 // 4, SEG_LEN, 1).astype(jnp.int32),
    }


exact_mode = lax.Precision.HIGHEST
soft_square = 0.1
ridge_term = 0.01
spectral_shift = 2.0

def featurize(frames, pairs):
    first_atom = jnp.take(frames, pairs[0], axis=2)
    second_atom = jnp.take(frames, pairs[1], axis=2)
    offset = first_atom - second_atom
    return jnp.sqrt(lax.optimization_barrier(jnp.sum(offset * offset, axis=1)) + soft_square)

def tri_solve(factor, rhs, transposed):
    return lax.linalg.triangular_solve(factor, rhs, left_side=True, lower=True, transpose_a=transposed)

def cross_gram(left_rows, right_rows):
    return lax.dot_general(left_rows.astype(jnp.float32), right_rows.astype(jnp.float32), (((0,), (0,)), ((), ())), precision=exact_mode, preferred_element_type=jnp.float32)

def subspace(c_zero, c_lag, basis_width):
    lower_factor = jnp.linalg.cholesky(c_zero)
    identity = jnp.eye(c_zero.shape[0], dtype=jnp.float32)
    basis_q = identity[:, :basis_width]
    for sweep in range(ITERS):
        inner_solve = tri_solve(lower_factor, basis_q, True)
        moved_block = jnp.dot(c_lag.astype(jnp.float32), inner_solve.astype(jnp.float32), precision=exact_mode, preferred_element_type=jnp.float32)
        image_block = tri_solve(lower_factor, moved_block, False) + spectral_shift * basis_q
        gram_small = cross_gram(image_block, image_block)
        small_factor = jnp.linalg.cholesky(gram_small)
        basis_q = tri_solve(small_factor, image_block.T, False).T
    return tri_solve(lower_factor, basis_q, True)

def reference(coords, pairs, lengths):
    frame_index = jnp.arange(SEG_LEN, dtype=jnp.int32)
    feature_count = pairs.shape[1]

    def masks_of(length):
        is_valid = (frame_index < length).astype(jnp.float32)
        paired = (frame_index + LAG < length).astype(jnp.float32)
        return (is_valid, paired)

    def lagged_of(features):
        return jnp.concatenate([features[LAG:], jnp.zeros((LAG, feature_count), jnp.float32)], axis=0)

    def first_pass(running, inputs):
        frames, length = inputs
        features = featurize(frames, pairs)
        is_valid, paired = masks_of(length)
        lagged = lagged_of(features)
        updated = (running[0] + jnp.sum(is_valid), running[1] + jnp.sum(paired), running[2] + jnp.dot(is_valid.astype(jnp.float32), features.astype(jnp.float32), precision=exact_mode, preferred_element_type=jnp.float32), running[3] + jnp.dot(paired.astype(jnp.float32), features.astype(jnp.float32), precision=exact_mode, preferred_element_type=jnp.float32), running[4] + jnp.dot(paired.astype(jnp.float32), lagged.astype(jnp.float32), precision=exact_mode, preferred_element_type=jnp.float32))
        return (updated, None)
    zero_scalar = jnp.zeros((), jnp.float32)
    zero_vector = jnp.zeros((feature_count,), jnp.float32)
    sums_out, unused = lax.scan(first_pass, (zero_scalar, zero_scalar, zero_vector, zero_vector, zero_vector), (coords, lengths))
    frames_total, pairs_total = (sums_out[0], sums_out[1])
    mean_all = sums_out[2] / frames_total
    mean_lead = sums_out[3] / pairs_total
    mean_ahead = sums_out[4] / pairs_total

    def second_pass(running, inputs):
        frames, length = inputs
        features = featurize(frames, pairs)
        is_valid, paired = masks_of(length)
        lagged = lagged_of(features)
        centered = (features - mean_all) * is_valid[:, None]
        lead_rows = (features - mean_lead) * paired[:, None]
        ahead_rows = (lagged - mean_ahead) * paired[:, None]
        return ((running[0] + cross_gram(centered, centered), running[1] + cross_gram(lead_rows, ahead_rows)), None)
    zero_matrix = jnp.zeros((feature_count, feature_count), jnp.float32)
    grams, unused = lax.scan(second_pass, (zero_matrix, zero_matrix), (coords, lengths))
    identity = jnp.eye(feature_count, dtype=jnp.float32)
    c_zero = grams[0] / frames_total + ridge_term * identity
    c_lag = (grams[1] + grams[1].T) / (2.0 * pairs_total)
    basis = subspace(c_zero, c_lag, K)

    def project(inputs):
        frames, length = inputs
        features = featurize(frames, pairs)
        is_valid, paired = masks_of(length)
        centered = (features - mean_all) * is_valid[:, None]
        return jnp.dot(centered.astype(jnp.float32), basis.astype(jnp.float32), precision=exact_mode, preferred_element_type=jnp.float32)
    return lax.map(project, (coords, lengths))
```

```python
import jax
import jax.numpy as jnp
from jax import lax
from jax.experimental import pallas as pl
from jax.experimental.pallas import tpu as pltpu
from jax.sharding import PartitionSpec as P

FEAT = 1024
K = 128
LAG = 10
ITERS = 3
TILE = 128
BLOCKS = FEAT // TILE
PANEL = 32

exact_mode = lax.Precision.HIGHEST
soft_square = 0.1
ridge_term = 0.01
spectral_shift = 2.0


def mm(a, b):
    return lax.dot_general(
        a, b, (((1,), (0,)), ((), ())), precision=exact_mode, preferred_element_type=jnp.float32
    )


def mm_t(a, b):
    return lax.dot_general(
        a, b, (((0,), (0,)), ((), ())), precision=exact_mode, preferred_element_type=jnp.float32
    )


def mm_nt(a, b):
    return lax.dot_general(
        a, b, (((1,), (1,)), ((), ())), precision=exact_mode, preferred_element_type=jnp.float32
    )


def inverse_factor(a):
    groups = [a[8 * g : 8 * g + 8, :] for g in range(16)]
    lane = lax.broadcasted_iota(jnp.int32, (8, TILE), 1)
    sub = lax.broadcasted_iota(jnp.int32, (8, TILE), 0)
    lane_one = lane[0:1, :]
    pivots = [jnp.ones((8, TILE), jnp.float32) for _ in range(16)]
    per = PANEL // 8
    for panel in range(TILE // PANEL):
        last = per * (panel + 1)
        for j in range(PANEL * panel, PANEL * (panel + 1)):
            home, at = j // 8, j % 8
            own = groups[home]
            column = jnp.broadcast_to(own[:, j : j + 1], (8, TILE))
            pivot = column[at : at + 1, :]
            inv = 1.0 / pivot
            scaled = jnp.where(lane_one == j, 1.0, own[at : at + 1, :]) * inv
            unit = jnp.where(sub == at, 1.0, 0.0)
            kept = jnp.where((lane == j) & (sub >= at), unit, own)
            groups[home] = kept - jnp.where(sub > at, column, 0.0) * scaled
            pivots[home] = jnp.where(sub == at, pivot, pivots[home])
            for g in range(home + 1, last):
                column = jnp.broadcast_to(groups[g][:, j : j + 1], (8, TILE))
                groups[g] = jnp.where(lane == j, 0.0, groups[g]) - column * scaled
        if last < 16:
            rows = jnp.concatenate(groups[last - per : last], axis=0)
            scale = jnp.concatenate(pivots[last - per : last], axis=0)
            here = lax.broadcasted_iota(jnp.int32, (PANEL, TILE), 0) + PANEL * panel
            across = lax.broadcasted_iota(jnp.int32, (PANEL, TILE), 1)
            done = (across > here) & (across < PANEL * (panel + 1))
            update = mm_t(rows, jnp.where(done, 0.0, rows / scale))
            inside = (lane >= PANEL * panel) & (lane < PANEL * (panel + 1))
            for g in range(last, 16):
                groups[g] = jnp.where(inside, 0.0, groups[g]) - update[8 * g : 8 * g + 8, :]
    out = []
    for g in range(16):
        root = lax.rsqrt(pivots[g])
        root = root * (1.5 - 0.5 * pivots[g] * root * root)
        out.append(jnp.where(lane <= sub + 8 * g, groups[g] * root, 0.0))
    return jnp.concatenate(out, axis=0)


def gram_body(x_ref, lag_ref, center_ref, valid_ref, paired_ref, stat_ref, out_ref):
    center = center_ref[0:1, :]
    valid = valid_ref[:, 0:1]
    paired = paired_ref[:, 0:1]
    base = x_ref[...] - center
    centered = base * valid
    lead = base * paired
    ahead = (lag_ref[...] - center) * paired
    left = jnp.concatenate([lead, ahead], axis=0)
    right = jnp.concatenate([ahead, lead], axis=0)
    sum_lead = jnp.sum(lead, axis=0, keepdims=True)
    sum_ahead = jnp.sum(ahead, axis=0, keepdims=True)
    row = lax.broadcasted_iota(jnp.int32, (8, FEAT), 0)
    stats = jnp.where(row == 1, sum_lead, jnp.where(row == 2, sum_ahead, stat_ref[...]))
    out_ref[:, 9, :, :] = jnp.zeros((BLOCKS, TILE, TILE), jnp.float32)
    for r in range(BLOCKS):
        lo = TILE * r
        upper = mm_t(centered[:, lo : lo + TILE], centered[:, lo:])
        for c in range(r, BLOCKS):
            out_ref[r, c, :, :] = upper[:, TILE * (c - r) : TILE * (c - r + 1)]
        lower = mm_t(left[:, lo : lo + TILE], right[:, : lo + TILE])
        for c in range(r):
            out_ref[r, c, :, :] = lower[:, TILE * c : TILE * (c + 1)]
        out_ref[r, 8, :, :] = lower[:, lo:]
        out_ref[r, 9, 0:8, :] = stats[:, lo : lo + TILE]


def solve_body(g_ref, x_ref, valid_ref, out_ref, m_ref, lag_ref, row_ref):
    def stat(kind):
        lo = 9 * TILE + 32 * kind
        return jnp.concatenate([g_ref[r, lo : lo + 32, :] for r in range(BLOCKS)], axis=1)

    sums, a_sum, b_sum, count, pair = stat(0), stat(1), stat(2), stat(3), stat(4)
    frames_total = jnp.sum(count, axis=0, keepdims=True)
    pairs_total = jnp.sum(pair, axis=0, keepdims=True)
    mean_all = jnp.sum(sums, axis=0, keepdims=True) / frames_total
    inv_pair = 1.0 / jnp.maximum(pair, 1.0)
    dev = sums / count - mean_all
    dev_a = dev + a_sum * inv_pair
    dev_b = dev + b_sum * inv_pair
    dev_a = dev_a - jnp.sum(pair * dev_a, axis=0, keepdims=True) / pairs_total
    dev_b = dev_b - jnp.sum(pair * dev_b, axis=0, keepdims=True) / pairs_total
    left_zero = dev * count
    left_lag = jnp.concatenate(
        [-a_sum * inv_pair, -b_sum * inv_pair, pair * dev_a, pair * dev_b], axis=0
    )
    right_lag = jnp.concatenate([b_sum, a_sum, dev_b, dev_a], axis=0)
    inv_frames = 1.0 / frames_total[:, :TILE]
    inv_pairs = 0.5 / pairs_total[:, :TILE]
    diagonal = lax.broadcasted_iota(jnp.int32, (TILE, TILE), 0) == lax.broadcasted_iota(
        jnp.int32, (TILE, TILE), 1
    )
    for r in range(BLOCKS):
        lo = TILE * r
        fix = mm_t(left_zero[:, lo : lo + TILE], dev[:, lo:])
        fix_lag = mm_t(left_lag[:, lo : lo + TILE], right_lag[:, : lo + TILE])
        for c in range(BLOCKS):
            at = TILE * c
            if c >= r:
                block = (g_ref[r, at : at + TILE, :] + fix[:, at - lo : at - lo + TILE]) * inv_frames
                if c == r:
                    block = jnp.where(diagonal, block + ridge_term, block)
                m_ref[lo : lo + TILE, at : at + TILE] = block
            else:
                m_ref[lo : lo + TILE, at : at + TILE] = jnp.zeros((TILE, TILE), jnp.float32)
            if c <= r:
                slot = 8 if c == r else c
                block = g_ref[r, TILE * slot : TILE * slot + TILE, :] + fix_lag[:, at : at + TILE]
                block = block * inv_pairs
                lag_ref[lo : lo + TILE, at : at + TILE] = block
                if c < r:
                    lag_ref[at : at + TILE, lo : lo + TILE] = block.T

    lane_all = lax.broadcasted_iota(jnp.int32, (TILE, FEAT), 1)

    def eliminate(k, carry):
        lo = pl.multiple_of(k * TILE, TILE)
        factor = inverse_factor(m_ref[pl.ds(lo, TILE), pl.ds(lo, TILE)])
        row_ref[...] = mm(factor, m_ref[pl.ds(lo, TILE), :])
        row_ref[:, pl.ds(lo, TILE)] = factor
        m_ref[pl.ds(lo, TILE), :] = row_ref[...]
        inside = (lane_all >= lo) & (lane_all < lo + TILE)

        def below(i, inner):
            at = pl.multiple_of(i * TILE, TILE)
            update = mm_t(row_ref[:, pl.ds(at, TILE)], row_ref[...])
            old = jnp.where(inside, 0.0, m_ref[pl.ds(at, TILE), :])
            m_ref[pl.ds(at, TILE), :] = old - update
            return inner

        return lax.fori_loop(k + 1, BLOCKS, below, carry)

    lax.fori_loop(0, BLOCKS, eliminate, 0)

    def solve_rows(q):
        return jnp.concatenate(
            [
                mm(m_ref[TILE * r : TILE * (r + 1), : TILE * (r + 1)], q[: TILE * (r + 1)])
                for r in range(BLOCKS)
            ],
            axis=0,
        )

    def solve_columns(q):
        return jnp.concatenate(
            [
                mm_t(m_ref[TILE * r :, TILE * r : TILE * (r + 1)], q[TILE * r :])
                for r in range(BLOCKS)
            ],
            axis=0,
        )

    def sweep(step, q):
        inner = solve_columns(q)
        return solve_rows(mm(lag_ref[...], inner)) + spectral_shift * q

    start = (
        lax.broadcasted_iota(jnp.int32, (FEAT, K), 0) == lax.broadcasted_iota(jnp.int32, (FEAT, K), 1)
    ).astype(jnp.float32)
    image = lax.fori_loop(0, ITERS, sweep, start)
    small = inverse_factor(mm_t(image, image))
    basis = mm_nt(solve_columns(image), small)
    shifted = (x_ref[...] - mean_all) * valid_ref[:, 0:1]
    out_ref[...] = mm(shifted, basis)


def gram_call(*args):
    return pl.pallas_call(
        gram_body,
        out_shape=jax.ShapeDtypeStruct((BLOCKS, 10, TILE, TILE), jnp.float32),
        compiler_params=pltpu.CompilerParams(vmem_limit_bytes=48 << 20),
        name="packed_scatter",
    )(*args)


def solve_call(*args):
    return pl.pallas_call(
        solve_body,
        out_shape=jax.ShapeDtypeStruct((TILE, K), jnp.float32),
        scratch_shapes=[
            pltpu.VMEM((FEAT, FEAT), jnp.float32),
            pltpu.VMEM((FEAT, FEAT), jnp.float32),
            pltpu.VMEM((TILE, FEAT), jnp.float32),
        ],
        compiler_params=pltpu.CompilerParams(vmem_limit_bytes=56 << 20),
        name="subspace",
    )(*args)


def featurize(frames, pairs):
    atoms = frames.shape[2]
    atom = lax.broadcasted_iota(jnp.int32, (atoms, FEAT), 0)
    pick = (atom == pairs[0:1]).astype(jnp.float32) - (atom == pairs[1:2]).astype(jnp.float32)
    offset = jnp.einsum(
        "tca,af->ctf", frames, pick, precision=exact_mode, preferred_element_type=jnp.float32
    )
    return jnp.sqrt(jnp.sum(offset * offset, axis=0) + soft_square)


def everywhere(x, axis, peers):
    return lax.all_to_all(jnp.broadcast_to(x[None], (peers,) + x.shape), axis, 0, 0)


def on_device(coords, pairs, lengths):
    segs = lax.axis_size("seg")
    trajs = lax.axis_size("traj")
    frames = coords[0]
    rows = frames.shape[0]
    features = featurize(frames, pairs)
    arriving = lax.ppermute(features[:LAG], "seg", [(i + 1, i) for i in range(segs - 1)])
    lagged = jnp.concatenate([features[LAG:], arriving], axis=0)
    index = lax.axis_index("seg") * rows + lax.broadcasted_iota(jnp.int32, (rows, TILE), 0)
    length = lengths[0]
    valid = (index < length).astype(jnp.float32)
    paired = (index + LAG < length).astype(jnp.float32)
    count = jnp.sum(valid[:, 0])
    pair_count = jnp.sum(paired[:, 0])
    sum_all = jnp.sum(features * valid[:, 0:1], axis=0)
    row = lax.broadcasted_iota(jnp.int32, (8, FEAT), 0)
    stat_rows = jnp.where(
        row == 0,
        sum_all,
        jnp.where(row == 3, count, jnp.where(row == 4, pair_count, 0.0)),
    )
    group = jnp.sum(everywhere(stat_rows, "seg", segs), axis=0)
    center = jnp.broadcast_to(group[0:1] / group[3:4], (8, FEAT))
    packed = gram_call(features, lagged, center, valid, paired, stat_rows)
    chunk = lax.psum_scatter(
        packed.reshape(BLOCKS * 10 * TILE, TILE), "seg", scatter_dimension=0, tiled=True
    )
    stats = chunk[9 * TILE : 9 * TILE + 8]
    sent = jnp.concatenate(
        [chunk.reshape(trajs, 40, TILE), jnp.broadcast_to(stats[None], (trajs, 8, TILE))], axis=1
    )
    taken = lax.all_to_all(sent, "traj", 0, 0)
    own = jnp.sum(taken[:, :40], axis=0)
    whole = everywhere(own, "traj", trajs).reshape(10 * TILE, TILE)[: 9 * TILE]
    group_stats = taken[:, 40:].transpose(1, 0, 2).reshape(8 * trajs, TILE)
    gathered = lax.all_gather(jnp.concatenate([whole, group_stats], axis=0), "seg", axis=0)
    projected = solve_call(gathered, features, valid)
    return projected[None]


def solution(mesh):
    return jax.shard_map(
        on_device,
        mesh=mesh,
        in_specs=(P("traj", "seg", None, None), P(), P("traj")),
        out_specs=P("traj", "seg", None),
        check_vma=False,
    )
```

```python
import jax
import jax.numpy as jnp
from jax import lax
from jax.experimental import pallas as pl
from jax.experimental.pallas import tpu as pltpu
from jax.sharding import PartitionSpec as P

FEAT = 1024
K = 128
LAG = 10
ITERS = 3
TILE = 128
BLOCKS = FEAT // TILE
PANEL = 32

exact_mode = lax.Precision.HIGHEST
soft_square = 0.1
ridge_term = 0.01
spectral_shift = 2.0


def mm(a, b):
    return lax.dot_general(
        a, b, (((1,), (0,)), ((), ())), precision=exact_mode, preferred_element_type=jnp.float32
    )


def mm_t(a, b):
    return lax.dot_general(
        a, b, (((0,), (0,)), ((), ())), precision=exact_mode, preferred_element_type=jnp.float32
    )


def mm_nt(a, b):
    return lax.dot_general(
        a, b, (((1,), (1,)), ((), ())), precision=exact_mode, preferred_element_type=jnp.float32
    )


def inverse_factor(a):
    groups = [a[8 * g : 8 * g + 8, :] for g in range(16)]
    lane = lax.broadcasted_iota(jnp.int32, (8, TILE), 1)
    sub = lax.broadcasted_iota(jnp.int32, (8, TILE), 0)
    lane_one = lane[0:1, :]
    pivots = [jnp.ones((8, TILE), jnp.float32) for _ in range(16)]
    per = PANEL // 8
    for panel in range(TILE // PANEL):
        last = per * (panel + 1)
        for home in range(last - per, last):
            base = 8 * home
            columns = [
                [jnp.broadcast_to(groups[g][:, base + q : base + q + 1], (8, TILE)) for q in range(8)]
                for g in range(home, last)
            ]
            for j in range(8):
                pivot = jnp.broadcast_to(columns[0][j][j : j + 1, :], (8, TILE))
                inv = 1.0 / pivot
                here = lane == base + j
                own = jnp.broadcast_to(groups[home][j : j + 1, :], (8, TILE))
                scaled = jnp.where(here, 1.0, own) * inv
                factors = [
                    jnp.broadcast_to(columns[0][q][j : j + 1, :], (8, TILE)) * inv
                    for q in range(j + 1, 8)
                ]
                pivots[home] = jnp.where(sub == j, pivot, pivots[home])
                for g in range(home, last):
                    column = columns[g - home][j]
                    if g == home:
                        unit = jnp.where(sub == j, 1.0, 0.0)
                        column = jnp.where(sub > j, column, 0.0)
                        kept = jnp.where(here & (sub >= j), unit, groups[g])
                    else:
                        kept = jnp.where(here, 0.0, groups[g])
                    groups[g] = kept - column * scaled
                    for q in range(j + 1, 8):
                        columns[g - home][q] = columns[g - home][q] - column * factors[q - j - 1]
        if last < 16:
            rows = jnp.concatenate(groups[last - per : last], axis=0)
            scale = jnp.concatenate(pivots[last - per : last], axis=0)
            here = lax.broadcasted_iota(jnp.int32, (PANEL, TILE), 0) + PANEL * panel
            across = lax.broadcasted_iota(jnp.int32, (PANEL, TILE), 1)
            done = (across > here) & (across < PANEL * (panel + 1))
            update = mm_t(rows, jnp.where(done, 0.0, rows / scale))
            inside = (lane >= PANEL * panel) & (lane < PANEL * (panel + 1))
            for g in range(last, 16):
                groups[g] = jnp.where(inside, 0.0, groups[g]) - update[8 * g : 8 * g + 8, :]
    out = []
    for g in range(16):
        root = lax.rsqrt(pivots[g])
        root = root * (1.5 - 0.5 * pivots[g] * root * root)
        out.append(jnp.where(lane <= sub + 8 * g, groups[g] * root, 0.0))
    return jnp.concatenate(out, axis=0)


def gram_body(x_ref, lag_ref, center_ref, valid_ref, paired_ref, stat_ref, out_ref):
    center = center_ref[0:1, :]
    valid = valid_ref[:, 0:1]
    paired = paired_ref[:, 0:1]
    base = x_ref[...] - center
    centered = base * valid
    lead = base * paired
    ahead = (lag_ref[...] - center) * paired
    left = jnp.concatenate([lead, ahead], axis=0)
    right = jnp.concatenate([ahead, lead], axis=0)
    sum_lead = jnp.sum(lead, axis=0, keepdims=True)
    sum_ahead = jnp.sum(ahead, axis=0, keepdims=True)
    row = lax.broadcasted_iota(jnp.int32, (8, FEAT), 0)
    stats = jnp.where(row == 1, sum_lead, jnp.where(row == 2, sum_ahead, stat_ref[...]))
    out_ref[:, 9, :, :] = jnp.zeros((BLOCKS, TILE, TILE), jnp.float32)
    for r in range(BLOCKS):
        lo = TILE * r
        upper = mm_t(centered[:, lo : lo + TILE], centered[:, lo:])
        for c in range(r, BLOCKS):
            out_ref[r, c, :, :] = upper[:, TILE * (c - r) : TILE * (c - r + 1)]
        lower = mm_t(left[:, lo : lo + TILE], right[:, : lo + TILE])
        for c in range(r):
            out_ref[r, c, :, :] = lower[:, TILE * c : TILE * (c + 1)]
        out_ref[r, 8, :, :] = lower[:, lo:]
        out_ref[r, 9, 0:8, :] = stats[:, lo : lo + TILE]


def solve_body(g_ref, x_ref, valid_ref, out_ref, m_ref, lag_ref, row_ref):
    def stat(kind):
        lo = 9 * TILE + 32 * kind
        return jnp.concatenate([g_ref[r, lo : lo + 32, :] for r in range(BLOCKS)], axis=1)

    sums, a_sum, b_sum, count, pair = stat(0), stat(1), stat(2), stat(3), stat(4)
    frames_total = jnp.sum(count, axis=0, keepdims=True)
    pairs_total = jnp.sum(pair, axis=0, keepdims=True)
    mean_all = jnp.sum(sums, axis=0, keepdims=True) / frames_total
    inv_pair = 1.0 / jnp.maximum(pair, 1.0)
    dev = sums / count - mean_all
    dev_a = dev + a_sum * inv_pair
    dev_b = dev + b_sum * inv_pair
    dev_a = dev_a - jnp.sum(pair * dev_a, axis=0, keepdims=True) / pairs_total
    dev_b = dev_b - jnp.sum(pair * dev_b, axis=0, keepdims=True) / pairs_total
    left_zero = dev * count
    left_lag = jnp.concatenate(
        [-a_sum * inv_pair, -b_sum * inv_pair, pair * dev_a, pair * dev_b], axis=0
    )
    right_lag = jnp.concatenate([b_sum, a_sum, dev_b, dev_a], axis=0)
    inv_frames = 1.0 / frames_total[:, :TILE]
    inv_pairs = 0.5 / pairs_total[:, :TILE]
    diagonal = lax.broadcasted_iota(jnp.int32, (TILE, TILE), 0) == lax.broadcasted_iota(
        jnp.int32, (TILE, TILE), 1
    )
    for r in range(BLOCKS):
        lo = TILE * r
        fix = mm_t(left_zero[:, lo : lo + TILE], dev[:, lo:])
        fix_lag = mm_t(left_lag[:, lo : lo + TILE], right_lag[:, : lo + TILE])
        for c in range(BLOCKS):
            at = TILE * c
            if c >= r:
                block = (g_ref[r, at : at + TILE, :] + fix[:, at - lo : at - lo + TILE]) * inv_frames
                if c == r:
                    block = jnp.where(diagonal, block + ridge_term, block)
                m_ref[lo : lo + TILE, at : at + TILE] = block
            else:
                m_ref[lo : lo + TILE, at : at + TILE] = jnp.zeros((TILE, TILE), jnp.float32)
            if c <= r:
                slot = 8 if c == r else c
                block = g_ref[r, TILE * slot : TILE * slot + TILE, :] + fix_lag[:, at : at + TILE]
                block = block * inv_pairs
                lag_ref[lo : lo + TILE, at : at + TILE] = block
                if c < r:
                    lag_ref[at : at + TILE, lo : lo + TILE] = block.T

    lane_all = lax.broadcasted_iota(jnp.int32, (TILE, FEAT), 1)

    def eliminate(k, carry):
        lo = pl.multiple_of(k * TILE, TILE)
        factor = inverse_factor(m_ref[pl.ds(lo, TILE), pl.ds(lo, TILE)])
        row_ref[...] = mm(factor, m_ref[pl.ds(lo, TILE), :])
        row_ref[:, pl.ds(lo, TILE)] = factor
        m_ref[pl.ds(lo, TILE), :] = row_ref[...]
        inside = (lane_all >= lo) & (lane_all < lo + TILE)

        def below(i, inner):
            at = pl.multiple_of(i * TILE, TILE)
            update = mm_t(row_ref[:, pl.ds(at, TILE)], row_ref[...])
            old = jnp.where(inside, 0.0, m_ref[pl.ds(at, TILE), :])
            m_ref[pl.ds(at, TILE), :] = old - update
            return inner

        return lax.fori_loop(k + 1, BLOCKS, below, carry)

    lax.fori_loop(0, BLOCKS, eliminate, 0)

    def solve_rows(q):
        return jnp.concatenate(
            [
                mm(m_ref[TILE * r : TILE * (r + 1), : TILE * (r + 1)], q[: TILE * (r + 1)])
                for r in range(BLOCKS)
            ],
            axis=0,
        )

    def solve_columns(q):
        return jnp.concatenate(
            [
                mm_t(m_ref[TILE * r :, TILE * r : TILE * (r + 1)], q[TILE * r :])
                for r in range(BLOCKS)
            ],
            axis=0,
        )

    def sweep(step, q):
        inner = solve_columns(q)
        return solve_rows(mm(lag_ref[...], inner)) + spectral_shift * q

    start = (
        lax.broadcasted_iota(jnp.int32, (FEAT, K), 0) == lax.broadcasted_iota(jnp.int32, (FEAT, K), 1)
    ).astype(jnp.float32)
    first = mm_nt(lag_ref[:, :TILE], m_ref[:TILE, :TILE])
    image = solve_rows(first) + spectral_shift * start
    image = lax.fori_loop(1, ITERS, sweep, image)
    small = inverse_factor(mm_t(image, image))
    basis = mm_nt(solve_columns(image), small)
    shifted = (x_ref[...] - mean_all) * valid_ref[:, 0:1]
    out_ref[...] = mm(shifted, basis)


def gram_call(*args):
    return pl.pallas_call(
        gram_body,
        out_shape=jax.ShapeDtypeStruct((BLOCKS, 10, TILE, TILE), jnp.float32),
        compiler_params=pltpu.CompilerParams(vmem_limit_bytes=48 << 20),
        name="packed_scatter",
    )(*args)


def solve_call(*args):
    return pl.pallas_call(
        solve_body,
        out_shape=jax.ShapeDtypeStruct((TILE, K), jnp.float32),
        scratch_shapes=[
            pltpu.VMEM((FEAT, FEAT), jnp.float32),
            pltpu.VMEM((FEAT, FEAT), jnp.float32),
            pltpu.VMEM((TILE, FEAT), jnp.float32),
        ],
        compiler_params=pltpu.CompilerParams(vmem_limit_bytes=56 << 20),
        name="subspace",
    )(*args)


def featurize(frames, pairs):
    atoms = frames.shape[2]
    atom = lax.broadcasted_iota(jnp.int32, (atoms, FEAT), 0)
    pick = (atom == pairs[0:1]).astype(jnp.float32) - (atom == pairs[1:2]).astype(jnp.float32)
    offset = jnp.einsum(
        "tca,af->ctf", frames, pick, precision=exact_mode, preferred_element_type=jnp.float32
    )
    return jnp.sqrt(jnp.sum(offset * offset, axis=0) + soft_square)


def everywhere(x, axis, peers):
    return lax.all_to_all(jnp.broadcast_to(x[None], (peers,) + x.shape), axis, 0, 0)


def on_device(coords, pairs, lengths):
    segs = lax.axis_size("seg")
    trajs = lax.axis_size("traj")
    frames = coords[0]
    rows = frames.shape[0]
    features = featurize(frames, pairs)
    arriving = lax.ppermute(features[:LAG], "seg", [(i + 1, i) for i in range(segs - 1)])
    lagged = jnp.concatenate([features[LAG:], arriving], axis=0)
    index = lax.axis_index("seg") * rows + lax.broadcasted_iota(jnp.int32, (rows, TILE), 0)
    length = lengths[0]
    valid = (index < length).astype(jnp.float32)
    paired = (index + LAG < length).astype(jnp.float32)
    count = jnp.sum(valid[:, 0])
    pair_count = jnp.sum(paired[:, 0])
    sum_all = jnp.sum(features * valid[:, 0:1], axis=0)
    row = lax.broadcasted_iota(jnp.int32, (8, FEAT), 0)
    stat_rows = jnp.where(
        row == 0,
        sum_all,
        jnp.where(row == 3, count, jnp.where(row == 4, pair_count, 0.0)),
    )
    group = jnp.sum(everywhere(stat_rows, "seg", segs), axis=0)
    center = jnp.broadcast_to(group[0:1] / group[3:4], (8, FEAT))
    packed = gram_call(features, lagged, center, valid, paired, stat_rows)
    chunk = lax.psum_scatter(
        packed.reshape(BLOCKS * 10 * TILE, TILE), "seg", scatter_dimension=0, tiled=True
    )
    stats = chunk[9 * TILE : 9 * TILE + 8]
    sent = jnp.concatenate(
        [chunk.reshape(trajs, 40, TILE), jnp.broadcast_to(stats[None], (trajs, 8, TILE))], axis=1
    )
    taken = lax.all_to_all(sent, "traj", 0, 0)
    own = jnp.sum(taken[:, :40], axis=0)
    whole = everywhere(own, "traj", trajs).reshape(10 * TILE, TILE)[: 9 * TILE]
    group_stats = taken[:, 40:].transpose(1, 0, 2).reshape(8 * trajs, TILE)
    gathered = lax.all_gather(jnp.concatenate([whole, group_stats], axis=0), "seg", axis=0)
    projected = solve_call(gathered, features, valid)
    return projected[None]


def solution(mesh):
    return jax.shard_map(
        on_device,
        mesh=mesh,
        in_specs=(P("traj", "seg", None, None), P(), P("traj")),
        out_specs=P("traj", "seg", None),
        check_vma=False,
    )
```

```python
import jax
import jax.numpy as jnp
from jax import lax
from jax.experimental import pallas as pl
from jax.experimental.pallas import tpu as pltpu
from jax.sharding import PartitionSpec as P

FEAT = 1024
K = 128
LAG = 10
ITERS = 3
TILE = 128
BLOCKS = FEAT // TILE
PANEL = 32
SLOTS = 5

exact_mode = lax.Precision.HIGHEST
soft_square = 0.1
ridge_term = 0.01
spectral_shift = 2.0


def mm(a, b):
    return lax.dot_general(
        a, b, (((1,), (0,)), ((), ())), precision=exact_mode, preferred_element_type=jnp.float32
    )


def mm_t(a, b):
    return lax.dot_general(
        a, b, (((0,), (0,)), ((), ())), precision=exact_mode, preferred_element_type=jnp.float32
    )


def mm_nt(a, b):
    return lax.dot_general(
        a, b, (((1,), (1,)), ((), ())), precision=exact_mode, preferred_element_type=jnp.float32
    )


def inverse_factor(a):
    groups = [a[8 * g : 8 * g + 8, :] for g in range(16)]
    lane = lax.broadcasted_iota(jnp.int32, (8, TILE), 1)
    sub = lax.broadcasted_iota(jnp.int32, (8, TILE), 0)
    lane_one = lane[0:1, :]
    pivots = [jnp.ones((8, TILE), jnp.float32) for _ in range(16)]
    per = PANEL // 8
    for panel in range(TILE // PANEL):
        last = per * (panel + 1)
        for home in range(last - per, last):
            base = 8 * home
            columns = [
                [jnp.broadcast_to(groups[g][:, base + q : base + q + 1], (8, TILE)) for q in range(8)]
                for g in range(home, last)
            ]
            for j in range(8):
                pivot = jnp.broadcast_to(columns[0][j][j : j + 1, :], (8, TILE))
                inv = 1.0 / pivot
                here = lane == base + j
                own = jnp.broadcast_to(groups[home][j : j + 1, :], (8, TILE))
                scaled = jnp.where(here, 1.0, own) * inv
                factors = [
                    jnp.broadcast_to(columns[0][q][j : j + 1, :], (8, TILE)) * inv
                    for q in range(j + 1, 8)
                ]
                pivots[home] = jnp.where(sub == j, pivot, pivots[home])
                for g in range(home, last):
                    column = columns[g - home][j]
                    if g == home:
                        unit = jnp.where(sub == j, 1.0, 0.0)
                        column = jnp.where(sub > j, column, 0.0)
                        kept = jnp.where(here & (sub >= j), unit, groups[g])
                    else:
                        kept = jnp.where(here, 0.0, groups[g])
                    groups[g] = kept - column * scaled
                    for q in range(j + 1, 8):
                        columns[g - home][q] = columns[g - home][q] - column * factors[q - j - 1]
        if last < 16:
            rows = jnp.concatenate(groups[last - per : last], axis=0)
            scale = jnp.concatenate(pivots[last - per : last], axis=0)
            here = lax.broadcasted_iota(jnp.int32, (PANEL, TILE), 0) + PANEL * panel
            across = lax.broadcasted_iota(jnp.int32, (PANEL, TILE), 1)
            done = (across > here) & (across < PANEL * (panel + 1))
            update = mm_t(rows, jnp.where(done, 0.0, rows / scale))
            inside = (lane >= PANEL * panel) & (lane < PANEL * (panel + 1))
            for g in range(last, 16):
                groups[g] = jnp.where(inside, 0.0, groups[g]) - update[8 * g : 8 * g + 8, :]
    out = []
    for g in range(16):
        root = lax.rsqrt(pivots[g])
        root = root * (1.5 - 0.5 * pivots[g] * root * root)
        out.append(jnp.where(lane <= sub + 8 * g, groups[g] * root, 0.0))
    return jnp.concatenate(out, axis=0)


def wrapped(x):
    return jnp.concatenate([x, x[:, : TILE * (SLOTS - 1)]], axis=1)


def zero_body(x_ref, lag_ref, center_ref, valid_ref, paired_ref, stat_ref, out_ref):
    center = center_ref[0:1, :]
    paired = paired_ref[:, 0:1]
    base = x_ref[...] - center
    centered = base * valid_ref[:, 0:1]
    sum_lead = jnp.sum(base * paired, axis=0, keepdims=True)
    sum_ahead = jnp.sum((lag_ref[...] - center) * paired, axis=0, keepdims=True)
    row = lax.broadcasted_iota(jnp.int32, (8, FEAT), 0)
    stats = jnp.where(row == 1, sum_lead, jnp.where(row == 2, sum_ahead, stat_ref[...]))
    out_ref[:, SLOTS, :, :] = jnp.zeros((BLOCKS, TILE, TILE), jnp.float32)
    right = wrapped(centered)
    for r in range(BLOCKS):
        lo = TILE * r
        part = mm_t(centered[:, lo : lo + TILE], right[:, lo : lo + TILE * SLOTS])
        for c in range(SLOTS):
            out_ref[r, c, :, :] = part[:, TILE * c : TILE * (c + 1)]
        out_ref[r, SLOTS, 0:8, :] = stats[:, lo : lo + TILE]


def lag_body(x_ref, lag_ref, center_ref, paired_ref, out_ref):
    center = center_ref[0:1, :]
    paired = paired_ref[:, 0:1]
    lead = (x_ref[...] - center) * paired
    ahead = (lag_ref[...] - center) * paired
    left = jnp.concatenate([lead, ahead], axis=0)
    right = wrapped(jnp.concatenate([ahead, lead], axis=0))
    for r in range(BLOCKS):
        lo = TILE * r
        part = mm_t(left[:, lo : lo + TILE], right[:, lo : lo + TILE * SLOTS])
        for c in range(SLOTS):
            out_ref[r, c, :, :] = part[:, TILE * c : TILE * (c + 1)]


def stat_of(g_ref, kind):
    lo = SLOTS * TILE + 32 * kind
    return jnp.concatenate([g_ref[r, lo : lo + 32, :] for r in range(BLOCKS)], axis=1)


def totals_of(g_ref):
    sums, count = stat_of(g_ref, 0), stat_of(g_ref, 3)
    frames_total = jnp.sum(count, axis=0, keepdims=True)
    mean_all = jnp.sum(sums, axis=0, keepdims=True) / frames_total
    return count, frames_total, mean_all, sums / count - mean_all


def held(r):
    return [(c, (r + c) % BLOCKS) for c in range(SLOTS) if c < SLOTS - 1 or r < BLOCKS // 2]


def factor_body(g_ref, m_ref, row_ref):
    count, frames_total, _, dev = totals_of(g_ref)
    left = dev * count
    right = wrapped(dev)
    inv_frames = 1.0 / frames_total[:, :TILE]
    diagonal = lax.broadcasted_iota(jnp.int32, (TILE, TILE), 0) == lax.broadcasted_iota(
        jnp.int32, (TILE, TILE), 1
    )
    for r in range(BLOCKS):
        lo = TILE * r
        fix = mm_t(left[:, lo : lo + TILE], right[:, lo : lo + TILE * SLOTS])
        for c, home in held(r):
            at = TILE * c
            block = (g_ref[r, at : at + TILE, :] + fix[:, at : at + TILE]) * inv_frames
            to = TILE * home
            if c == 0:
                block = jnp.where(diagonal, block + ridge_term, block)
            if home < r:
                m_ref[to : to + TILE, lo : lo + TILE] = block.T
                m_ref[lo : lo + TILE, to : to + TILE] = jnp.zeros((TILE, TILE), jnp.float32)
            else:
                m_ref[lo : lo + TILE, to : to + TILE] = block
                if home > r:
                    m_ref[to : to + TILE, lo : lo + TILE] = jnp.zeros((TILE, TILE), jnp.float32)

    lane_all = lax.broadcasted_iota(jnp.int32, (TILE, FEAT), 1)

    def eliminate(k, carry):
        lo = pl.multiple_of(k * TILE, TILE)
        factor = inverse_factor(m_ref[pl.ds(lo, TILE), pl.ds(lo, TILE)])
        row_ref[...] = mm(factor, m_ref[pl.ds(lo, TILE), :])
        row_ref[:, pl.ds(lo, TILE)] = factor
        m_ref[pl.ds(lo, TILE), :] = row_ref[...]
        inside = (lane_all >= lo) & (lane_all < lo + TILE)

        def below(i, inner):
            at = pl.multiple_of(i * TILE, TILE)
            update = mm_t(row_ref[:, pl.ds(at, TILE)], row_ref[...])
            old = jnp.where(inside, 0.0, m_ref[pl.ds(at, TILE), :])
            m_ref[pl.ds(at, TILE), :] = old - update
            return inner

        return lax.fori_loop(k + 1, BLOCKS, below, carry)

    lax.fori_loop(0, BLOCKS, eliminate, 0)


def sweep_body(m_ref, g_ref, lag_in_ref, x_ref, valid_ref, out_ref, lag_ref):
    _, _, mean_all, dev = totals_of(g_ref)
    a_sum, b_sum, pair = stat_of(g_ref, 1), stat_of(g_ref, 2), stat_of(g_ref, 4)
    pairs_total = jnp.sum(pair, axis=0, keepdims=True)
    inv_pair = 1.0 / jnp.maximum(pair, 1.0)
    dev_a = dev + a_sum * inv_pair
    dev_b = dev + b_sum * inv_pair
    dev_a = dev_a - jnp.sum(pair * dev_a, axis=0, keepdims=True) / pairs_total
    dev_b = dev_b - jnp.sum(pair * dev_b, axis=0, keepdims=True) / pairs_total
    left = jnp.concatenate(
        [-a_sum * inv_pair, -b_sum * inv_pair, pair * dev_a, pair * dev_b], axis=0
    )
    right = wrapped(jnp.concatenate([b_sum, a_sum, dev_b, dev_a], axis=0))
    inv_pairs = 0.5 / pairs_total[:, :TILE]
    for r in range(BLOCKS):
        lo = TILE * r
        fix = mm_t(left[:, lo : lo + TILE], right[:, lo : lo + TILE * SLOTS])
        for c, home in held(r):
            at, to = TILE * c, TILE * home
            block = (lag_in_ref[r, at : at + TILE, :] + fix[:, at : at + TILE]) * inv_pairs
            lag_ref[lo : lo + TILE, to : to + TILE] = block
            if c:
                lag_ref[to : to + TILE, lo : lo + TILE] = block.T

    def solve_rows(q):
        return jnp.concatenate(
            [
                mm(m_ref[TILE * r : TILE * (r + 1), : TILE * (r + 1)], q[: TILE * (r + 1)])
                for r in range(BLOCKS)
            ],
            axis=0,
        )

    def solve_columns(q):
        return jnp.concatenate(
            [
                mm_t(m_ref[TILE * r :, TILE * r : TILE * (r + 1)], q[TILE * r :])
                for r in range(BLOCKS)
            ],
            axis=0,
        )

    def sweep(step, q):
        inner = solve_columns(q)
        return solve_rows(mm(lag_ref[...], inner)) + spectral_shift * q

    start = (
        lax.broadcasted_iota(jnp.int32, (FEAT, K), 0) == lax.broadcasted_iota(jnp.int32, (FEAT, K), 1)
    ).astype(jnp.float32)
    first = mm_nt(lag_ref[:, :TILE], m_ref[:TILE, :TILE])
    image = solve_rows(first) + spectral_shift * start
    image = lax.fori_loop(1, ITERS, sweep, image)
    small = inverse_factor(mm_t(image, image))
    basis = mm_nt(solve_columns(image), small)
    shifted = (x_ref[...] - mean_all) * valid_ref[:, 0:1]
    out_ref[...] = mm(shifted, basis)


def zero_call(*args):
    return pl.pallas_call(
        zero_body,
        out_shape=jax.ShapeDtypeStruct((BLOCKS, SLOTS + 1, TILE, TILE), jnp.float32),
        compiler_params=pltpu.CompilerParams(vmem_limit_bytes=32 << 20),
        name="scatter_zero",
    )(*args)


def lag_call(*args):
    return pl.pallas_call(
        lag_body,
        out_shape=jax.ShapeDtypeStruct((BLOCKS, SLOTS, TILE, TILE), jnp.float32),
        compiler_params=pltpu.CompilerParams(vmem_limit_bytes=32 << 20),
        name="scatter_lag",
    )(*args)


def factor_call(*args):
    return pl.pallas_call(
        factor_body,
        out_shape=jax.ShapeDtypeStruct((FEAT, FEAT), jnp.float32),
        scratch_shapes=[pltpu.VMEM((TILE, FEAT), jnp.float32)],
        compiler_params=pltpu.CompilerParams(vmem_limit_bytes=32 << 20),
        name="factor",
    )(*args)


def sweep_call(*args):
    return pl.pallas_call(
        sweep_body,
        out_shape=jax.ShapeDtypeStruct((TILE, K), jnp.float32),
        scratch_shapes=[pltpu.VMEM((FEAT, FEAT), jnp.float32)],
        compiler_params=pltpu.CompilerParams(vmem_limit_bytes=40 << 20),
        name="sweeps",
    )(*args)


def featurize(frames, pairs):
    atoms = frames.shape[2]
    atom = lax.broadcasted_iota(jnp.int32, (atoms, FEAT), 0)
    pick = (atom == pairs[0:1]).astype(jnp.float32) - (atom == pairs[1:2]).astype(jnp.float32)
    offset = jnp.einsum(
        "tca,af->ctf", frames, pick, precision=exact_mode, preferred_element_type=jnp.float32
    )
    return jnp.sqrt(jnp.sum(offset * offset, axis=0) + soft_square)


def everywhere(x, axis, peers):
    return lax.all_to_all(jnp.broadcast_to(x[None], (peers,) + x.shape), axis, 0, 0)


def on_device(coords, pairs, lengths):
    segs = lax.axis_size("seg")
    trajs = lax.axis_size("traj")
    frames = coords[0]
    rows = frames.shape[0]
    features = featurize(frames, pairs)
    arriving = lax.ppermute(features[:LAG], "seg", [(i + 1, i) for i in range(segs - 1)])
    lagged = jnp.concatenate([features[LAG:], arriving], axis=0)
    index = lax.axis_index("seg") * rows + lax.broadcasted_iota(jnp.int32, (rows, TILE), 0)
    length = lengths[0]
    valid = (index < length).astype(jnp.float32)
    paired = (index + LAG < length).astype(jnp.float32)
    count = jnp.sum(valid[:, 0])
    pair_count = jnp.sum(paired[:, 0])
    sum_all = jnp.sum(features * valid[:, 0:1], axis=0)
    row = lax.broadcasted_iota(jnp.int32, (8, FEAT), 0)
    stat_rows = jnp.where(
        row == 0,
        sum_all,
        jnp.where(row == 3, count, jnp.where(row == 4, pair_count, 0.0)),
    )
    group = jnp.sum(everywhere(stat_rows, "seg", segs), axis=0)
    center = jnp.broadcast_to(group[0:1] / group[3:4], (8, FEAT))
    flat = (SLOTS + 1) * TILE
    zero = zero_call(features, lagged, center, valid, paired, stat_rows)
    zero = lax.psum_scatter(zero.reshape(BLOCKS * flat, TILE), "seg", scatter_dimension=0, tiled=True)
    later = lag_call(features, lagged, center, paired)
    later = lax.psum_scatter(
        later.reshape(BLOCKS * SLOTS * TILE, TILE), "seg", scatter_dimension=0, tiled=True
    )
    stats = zero[SLOTS * TILE : SLOTS * TILE + 8]
    piece = flat // trajs
    sent = jnp.concatenate(
        [zero.reshape(trajs, piece, TILE), jnp.broadcast_to(stats[None], (trajs, 8, TILE))], axis=1
    )
    taken = lax.all_to_all(sent, "traj", 0, 0)
    own = jnp.sum(taken[:, :piece], axis=0)
    whole = everywhere(own, "traj", trajs).reshape(flat, TILE)[: SLOTS * TILE]
    group_stats = taken[:, piece:].transpose(1, 0, 2).reshape(8 * trajs, TILE)
    gathered = lax.all_gather(jnp.concatenate([whole, group_stats], axis=0), "seg", axis=0)
    later = lax.all_to_all(later.reshape(trajs, SLOTS * TILE // trajs, TILE), "traj", 0, 0)
    later = everywhere(jnp.sum(later, axis=0), "traj", trajs).reshape(SLOTS * TILE, TILE)
    gathered, later = lax.optimization_barrier((gathered, later))
    gathered_lag = lax.all_gather(later, "seg", axis=0)
    inverse = factor_call(gathered)
    projected = sweep_call(inverse, gathered, gathered_lag, features, valid)
    return projected[None]


def solution(mesh):
    return jax.shard_map(
        on_device,
        mesh=mesh,
        in_specs=(P("traj", "seg", None, None), P(), P("traj")),
        out_specs=P("traj", "seg", None),
        check_vma=False,
    )
```

```python
import jax
import jax.numpy as jnp
from jax import lax
from jax.experimental import pallas as pl
from jax.experimental.pallas import tpu as pltpu
from jax.sharding import PartitionSpec as P

FEAT = 1024
K = 128
LAG = 10
ITERS = 3
TILE = 128
BLOCKS = FEAT // TILE
PANEL = 32
SLOTS = 5

exact_mode = lax.Precision.HIGHEST
soft_square = 0.1
ridge_term = 0.01
spectral_shift = 2.0


def mm(a, b):
    return lax.dot_general(
        a, b, (((1,), (0,)), ((), ())), precision=exact_mode, preferred_element_type=jnp.float32
    )


def mm_t(a, b):
    return lax.dot_general(
        a, b, (((0,), (0,)), ((), ())), precision=exact_mode, preferred_element_type=jnp.float32
    )


def mm_nt(a, b):
    return lax.dot_general(
        a, b, (((1,), (1,)), ((), ())), precision=exact_mode, preferred_element_type=jnp.float32
    )


def inverse_factor(a):
    groups = [a[8 * g : 8 * g + 8, :] for g in range(16)]
    lane = lax.broadcasted_iota(jnp.int32, (8, TILE), 1)
    sub = lax.broadcasted_iota(jnp.int32, (8, TILE), 0)
    lane_one = lane[0:1, :]
    pivots = [jnp.ones((8, TILE), jnp.float32) for _ in range(16)]
    per = PANEL // 8
    for panel in range(TILE // PANEL):
        last = per * (panel + 1)
        for home in range(last - per, last):
            base = 8 * home
            columns = [
                [jnp.broadcast_to(groups[g][:, base + q : base + q + 1], (8, TILE)) for q in range(8)]
                for g in range(home, last)
            ]
            for j in range(8):
                pivot = jnp.broadcast_to(columns[0][j][j : j + 1, :], (8, TILE))
                inv = 1.0 / pivot
                here = lane == base + j
                own = jnp.broadcast_to(groups[home][j : j + 1, :], (8, TILE))
                scaled = jnp.where(here, 1.0, own) * inv
                factors = [
                    jnp.broadcast_to(columns[0][q][j : j + 1, :], (8, TILE)) * inv
                    for q in range(j + 1, 8)
                ]
                pivots[home] = jnp.where(sub == j, pivot, pivots[home])
                for g in range(home, last):
                    column = columns[g - home][j]
                    if g == home:
                        unit = jnp.where(sub == j, 1.0, 0.0)
                        column = jnp.where(sub > j, column, 0.0)
                        kept = jnp.where(here & (sub >= j), unit, groups[g])
                    else:
                        kept = jnp.where(here, 0.0, groups[g])
                    groups[g] = kept - column * scaled
                    for q in range(j + 1, 8):
                        columns[g - home][q] = columns[g - home][q] - column * factors[q - j - 1]
        if last < 16:
            rows = jnp.concatenate(groups[last - per : last], axis=0)
            scale = jnp.concatenate(pivots[last - per : last], axis=0)
            here = lax.broadcasted_iota(jnp.int32, (PANEL, TILE), 0) + PANEL * panel
            across = lax.broadcasted_iota(jnp.int32, (PANEL, TILE), 1)
            done = (across > here) & (across < PANEL * (panel + 1))
            update = mm_t(rows, jnp.where(done, 0.0, rows / scale))
            inside = (lane >= PANEL * panel) & (lane < PANEL * (panel + 1))
            for g in range(last, 16):
                groups[g] = jnp.where(inside, 0.0, groups[g]) - update[8 * g : 8 * g + 8, :]
    out = []
    for g in range(16):
        root = lax.rsqrt(pivots[g])
        root = root * (1.5 - 0.5 * pivots[g] * root * root)
        out.append(jnp.where(lane <= sub + 8 * g, groups[g] * root, 0.0))
    return jnp.concatenate(out, axis=0)


def wrapped(x):
    return jnp.concatenate([x, x[:, : TILE * (SLOTS - 1)]], axis=1)


def zero_body(x_ref, lag_ref, center_ref, valid_ref, paired_ref, stat_ref, out_ref):
    center = center_ref[0:1, :]
    paired = paired_ref[:, 0:1]
    base = x_ref[...] - center
    centered = base * valid_ref[:, 0:1]
    sum_lead = jnp.sum(base * paired, axis=0, keepdims=True)
    sum_ahead = jnp.sum((lag_ref[...] - center) * paired, axis=0, keepdims=True)
    row = lax.broadcasted_iota(jnp.int32, (8, FEAT), 0)
    stats = jnp.where(row == 1, sum_lead, jnp.where(row == 2, sum_ahead, stat_ref[...]))
    out_ref[:, SLOTS, :, :] = jnp.zeros((BLOCKS, TILE, TILE), jnp.float32)
    right = wrapped(centered)
    for r in range(BLOCKS):
        lo = TILE * r
        part = mm_t(centered[:, lo : lo + TILE], right[:, lo : lo + TILE * SLOTS])
        for c in range(SLOTS):
            out_ref[r, c, :, :] = part[:, TILE * c : TILE * (c + 1)]
        out_ref[r, SLOTS, 0:8, :] = stats[:, lo : lo + TILE]


def lag_body(x_ref, lag_ref, center_ref, paired_ref, out_ref, left_ref, right_ref):
    center = center_ref[0:1, :]
    paired = paired_ref[:, 0:1]
    lead = (x_ref[...] - center) * paired
    ahead = (lag_ref[...] - center) * paired
    left_ref[...] = jnp.concatenate([lead, ahead], axis=0)
    right_ref[...] = wrapped(jnp.concatenate([ahead, lead], axis=0))

    def block_row(r, carry):
        lo = pl.multiple_of(r * TILE, TILE)
        part = mm_t(left_ref[:, pl.ds(lo, TILE)], right_ref[:, pl.ds(lo, TILE * SLOTS)])
        for c in range(SLOTS):
            out_ref[r, c, :, :] = part[:, TILE * c : TILE * (c + 1)]
        return carry

    lax.fori_loop(0, BLOCKS, block_row, 0)


def stat_of(g_ref, kind):
    lo = SLOTS * TILE + 32 * kind
    return jnp.concatenate([g_ref[r, lo : lo + 32, :] for r in range(BLOCKS)], axis=1)


def totals_of(g_ref):
    sums, count = stat_of(g_ref, 0), stat_of(g_ref, 3)
    frames_total = jnp.sum(count, axis=0, keepdims=True)
    mean_all = jnp.sum(sums, axis=0, keepdims=True) / frames_total
    return count, frames_total, mean_all, sums / count - mean_all


def held(r):
    return [(c, (r + c) % BLOCKS) for c in range(SLOTS) if c < SLOTS - 1 or r < BLOCKS // 2]


def factor_body(g_ref, m_ref, stats_ref, row_ref):
    for i in range(5):
        stats_ref[32 * i : 32 * i + 32, :] = stat_of(g_ref, i)
    count, frames_total, _, dev = totals_of(g_ref)
    left = dev * count
    right = wrapped(dev)
    inv_frames = 1.0 / frames_total[:, :TILE]
    diagonal = lax.broadcasted_iota(jnp.int32, (TILE, TILE), 0) == lax.broadcasted_iota(
        jnp.int32, (TILE, TILE), 1
    )
    for r in range(BLOCKS):
        lo = TILE * r
        fix = mm_t(left[:, lo : lo + TILE], right[:, lo : lo + TILE * SLOTS])
        for c, home in held(r):
            at = TILE * c
            block = (g_ref[r, at : at + TILE, :] + fix[:, at : at + TILE]) * inv_frames
            to = TILE * home
            if c == 0:
                block = jnp.where(diagonal, block + ridge_term, block)
            if home < r:
                m_ref[to : to + TILE, lo : lo + TILE] = block.T
                m_ref[lo : lo + TILE, to : to + TILE] = jnp.zeros((TILE, TILE), jnp.float32)
            else:
                m_ref[lo : lo + TILE, to : to + TILE] = block
                if home > r:
                    m_ref[to : to + TILE, lo : lo + TILE] = jnp.zeros((TILE, TILE), jnp.float32)

    lane_all = lax.broadcasted_iota(jnp.int32, (TILE, FEAT), 1)

    def eliminate(k, carry):
        lo = pl.multiple_of(k * TILE, TILE)
        factor = inverse_factor(m_ref[pl.ds(lo, TILE), pl.ds(lo, TILE)])
        row_ref[...] = mm(factor, m_ref[pl.ds(lo, TILE), :])
        row_ref[:, pl.ds(lo, TILE)] = factor
        m_ref[pl.ds(lo, TILE), :] = row_ref[...]
        inside = (lane_all >= lo) & (lane_all < lo + TILE)

        def below(i, inner):
            at = pl.multiple_of(i * TILE, TILE)
            update = mm_t(row_ref[:, pl.ds(at, TILE)], row_ref[...])
            old = jnp.where(inside, 0.0, m_ref[pl.ds(at, TILE), :])
            m_ref[pl.ds(at, TILE), :] = old - update
            return inner

        return lax.fori_loop(k + 1, BLOCKS, below, carry)

    lax.fori_loop(0, BLOCKS, eliminate, 0)


def sweep_body(
    m_ref, stats_ref, lag_in_ref, x_ref, valid_ref, out_ref, lag_ref, q_ref, moved_ref, inner_ref
):
    sums, a_sum, b_sum, count, pair = [stats_ref[32 * i : 32 * i + 32, :] for i in range(5)]
    mean_all = jnp.sum(sums, axis=0, keepdims=True) / jnp.sum(count, axis=0, keepdims=True)
    dev = sums / count - mean_all
    pairs_total = jnp.sum(pair, axis=0, keepdims=True)
    inv_pair = 1.0 / jnp.maximum(pair, 1.0)
    dev_a = dev + a_sum * inv_pair
    dev_b = dev + b_sum * inv_pair
    dev_a = dev_a - jnp.sum(pair * dev_a, axis=0, keepdims=True) / pairs_total
    dev_b = dev_b - jnp.sum(pair * dev_b, axis=0, keepdims=True) / pairs_total
    left = jnp.concatenate(
        [-a_sum * inv_pair, -b_sum * inv_pair, pair * dev_a, pair * dev_b], axis=0
    )
    right = wrapped(jnp.concatenate([b_sum, a_sum, dev_b, dev_a], axis=0))
    inv_pairs = 0.5 / pairs_total[:, :TILE]
    for r in range(BLOCKS):
        lo = TILE * r
        fix = mm_t(left[:, lo : lo + TILE], right[:, lo : lo + TILE * SLOTS])
        for c, home in held(r):
            at, to = TILE * c, TILE * home
            block = (lag_in_ref[r, at : at + TILE, :] + fix[:, at : at + TILE]) * inv_pairs
            lag_ref[lo : lo + TILE, to : to + TILE] = block
            if c:
                lag_ref[to : to + TILE, lo : lo + TILE] = block.T

    def solve_rows(q):
        return jnp.concatenate(
            [
                mm(m_ref[TILE * r : TILE * (r + 1), : TILE * (r + 1)], q[: TILE * (r + 1)])
                for r in range(BLOCKS)
            ],
            axis=0,
        )

    def solve_columns(q):
        return jnp.concatenate(
            [
                mm_t(m_ref[TILE * r :, TILE * r : TILE * (r + 1)], q[TILE * r :])
                for r in range(BLOCKS)
            ],
            axis=0,
        )

    q_ref[...] = (
        lax.broadcasted_iota(jnp.int32, (FEAT, K), 0) == lax.broadcasted_iota(jnp.int32, (FEAT, K), 1)
    ).astype(jnp.float32)
    moved_ref[...] = mm_nt(lag_ref[:, :TILE], m_ref[:TILE, :TILE])

    def sweep(step, carry):
        image = solve_rows(moved_ref[...]) + spectral_shift * q_ref[...]
        q_ref[...] = image
        inner_ref[...] = solve_columns(image)

        @pl.when(step < ITERS - 1)
        def _():
            moved_ref[...] = mm(lag_ref[...], inner_ref[...])

        return carry

    lax.fori_loop(0, ITERS, sweep, 0)
    image = q_ref[...]
    small = inverse_factor(mm_t(image, image))
    basis = mm_nt(inner_ref[...], small)
    shifted = (x_ref[...] - mean_all) * valid_ref[:, 0:1]
    out_ref[...] = mm(shifted, basis)


def zero_call(*args):
    return pl.pallas_call(
        zero_body,
        out_shape=jax.ShapeDtypeStruct((BLOCKS, SLOTS + 1, TILE, TILE), jnp.float32),
        compiler_params=pltpu.CompilerParams(vmem_limit_bytes=32 << 20),
        name="scatter_zero",
    )(*args)


def lag_call(*args):
    return pl.pallas_call(
        lag_body,
        out_shape=jax.ShapeDtypeStruct((BLOCKS, SLOTS, TILE, TILE), jnp.float32),
        scratch_shapes=[
            pltpu.VMEM((2 * TILE, FEAT), jnp.float32),
            pltpu.VMEM((2 * TILE, FEAT + TILE * (SLOTS - 1)), jnp.float32),
        ],
        compiler_params=pltpu.CompilerParams(vmem_limit_bytes=32 << 20),
        name="scatter_lag",
    )(*args)


def factor_call(*args):
    return pl.pallas_call(
        factor_body,
        out_shape=(
            jax.ShapeDtypeStruct((FEAT, FEAT), jnp.float32),
            jax.ShapeDtypeStruct((160, FEAT), jnp.float32),
        ),
        scratch_shapes=[pltpu.VMEM((TILE, FEAT), jnp.float32)],
        compiler_params=pltpu.CompilerParams(vmem_limit_bytes=32 << 20),
        name="factor",
    )(*args)


def sweep_call(*args):
    return pl.pallas_call(
        sweep_body,
        out_shape=jax.ShapeDtypeStruct((TILE, K), jnp.float32),
        scratch_shapes=[pltpu.VMEM((FEAT, FEAT), jnp.float32)]
        + [pltpu.VMEM((FEAT, K), jnp.float32) for _ in range(3)],
        compiler_params=pltpu.CompilerParams(vmem_limit_bytes=40 << 20),
        name="sweeps",
    )(*args)


def featurize(frames, pairs):
    atoms = frames.shape[2]
    atom = lax.broadcasted_iota(jnp.int32, (atoms, FEAT), 0)
    pick = (atom == pairs[0:1]).astype(jnp.float32) - (atom == pairs[1:2]).astype(jnp.float32)
    offset = jnp.einsum(
        "tca,af->ctf", frames, pick, precision=exact_mode, preferred_element_type=jnp.float32
    )
    return jnp.sqrt(jnp.sum(offset * offset, axis=0) + soft_square)


def everywhere(x, axis, peers):
    return lax.all_to_all(jnp.broadcast_to(x[None], (peers,) + x.shape), axis, 0, 0)


def on_device(coords, pairs, lengths):
    segs = lax.axis_size("seg")
    trajs = lax.axis_size("traj")
    frames = coords[0]
    rows = frames.shape[0]
    features = featurize(frames, pairs)
    arriving = lax.ppermute(features[:LAG], "seg", [(i + 1, i) for i in range(segs - 1)])
    lagged = jnp.concatenate([features[LAG:], arriving], axis=0)
    index = lax.axis_index("seg") * rows + lax.broadcasted_iota(jnp.int32, (rows, TILE), 0)
    length = lengths[0]
    valid = (index < length).astype(jnp.float32)
    paired = (index + LAG < length).astype(jnp.float32)
    count = jnp.sum(valid[:, 0])
    pair_count = jnp.sum(paired[:, 0])
    sum_all = jnp.sum(features * valid[:, 0:1], axis=0)
    row = lax.broadcasted_iota(jnp.int32, (8, FEAT), 0)
    stat_rows = jnp.where(
        row == 0,
        sum_all,
        jnp.where(row == 3, count, jnp.where(row == 4, pair_count, 0.0)),
    )
    group = jnp.sum(everywhere(stat_rows, "seg", segs), axis=0)
    center = jnp.broadcast_to(group[0:1] / group[3:4], (8, FEAT))
    flat = (SLOTS + 1) * TILE
    zero = zero_call(features, lagged, center, valid, paired, stat_rows)
    zero = lax.psum_scatter(zero.reshape(BLOCKS * flat, TILE), "seg", scatter_dimension=0, tiled=True)
    later = lag_call(features, lagged, center, paired)
    later = lax.psum_scatter(
        later.reshape(BLOCKS * SLOTS * TILE, TILE), "seg", scatter_dimension=0, tiled=True
    )
    stats = zero[SLOTS * TILE : SLOTS * TILE + 8]
    piece = flat // trajs
    sent = jnp.concatenate(
        [zero.reshape(trajs, piece, TILE), jnp.broadcast_to(stats[None], (trajs, 8, TILE))], axis=1
    )
    taken = lax.all_to_all(sent, "traj", 0, 0)
    own = jnp.sum(taken[:, :piece], axis=0)
    whole = everywhere(own, "traj", trajs).reshape(flat, TILE)[: SLOTS * TILE]
    group_stats = taken[:, piece:].transpose(1, 0, 2).reshape(8 * trajs, TILE)
    gathered = lax.all_gather(jnp.concatenate([whole, group_stats], axis=0), "seg", axis=0)
    later = lax.all_to_all(later.reshape(trajs, SLOTS * TILE // trajs, TILE), "traj", 0, 0)
    later = everywhere(jnp.sum(later, axis=0), "traj", trajs).reshape(SLOTS * TILE, TILE)
    gathered, later = lax.optimization_barrier((gathered, later))
    gathered_lag = lax.all_gather(later, "seg", axis=0)
    inverse, all_stats = factor_call(gathered)
    projected = sweep_call(inverse, all_stats, gathered_lag, features, valid)
    return projected[None]


def solution(mesh):
    return jax.shard_map(
        on_device,
        mesh=mesh,
        in_specs=(P("traj", "seg", None, None), P(), P("traj")),
        out_specs=P("traj", "seg", None),
        check_vma=False,
    )
```
